32 devices in a mesh: group: 8 (over z, x), member: 4 (over y, core).
Axes of the slice: x: 2, y: 2, z: 4, core: 2. Of those that a mesh axis runs over, the one named last changes fastest.
Arguments:
- particles: float32 [8, 65536], P(None, ('group', 'member')), may hold values from 0 to 20, as said below
- new_slot: int32 [512], P(('group', 'member')), may hold values from 0 to 511, as said below
- neighbours: int32 [512, 6], P(('group', 'member')), may hold values from 0 to 23, as said below
- ghosts: int32 [32, 2], P(('group', 'member')), may hold values from 0 to 4, as said below
Outputs:
- energy: float32 [65536], P(('group', 'member'))
- density: float32 [65536], P(('group', 'member'))
The draws below stay inside these ranges and needn't reach their ends.
Inputs may be any that keep to these rules, and one draw needn't show every extreme that they name: A permutation of 0 to 511. Tile t goes to segment new_slot[t] // 16, where segment number = group index * 4 + member index; a tile keeps its member index. Every segment receives 16 tiles, no segment sends more than 4 tiles to one segment, and some segment sends exactly 4 tiles to one segment. `ghosts`: row d holds the number of tiles that segment d takes from the end of segment d - 1 and from the start of segment d + 1. Both are at least 1 except the first segment's left count and the last segment's right count, which are 0; some segment takes exactly 4 tiles from its left neighbour. `neighbours`: for moved tile s of segment d, entries count along the extended range: the last ghosts[d, 0] tiles of segment d - 1, then the 16 tiles of segment d, then the first ghosts[d, 1] tiles of segment d + 1; every entry lies inside that range, entry 0 is the tile itself, and entries may repeat. `particles`: Rows: positions within 0 to 1, masses within 0.5 / 768 to 2 / 768, smoothing lengths within 0.3 to 0.5, initial energies within 0.5 to 4, opacities within 0.05 to 20, heating within 0 to 1.
All inputs are finite; a program needn't handle non-finite values.
Results may differ from the reference program's by a relative error of at most 0.00014.
Values sent between devices are 32-bit elements; how exact they have to be, the bound alone decides.
A program may use at most 64 MiB of HBM per device.

```python
import math
import jax
import jax.numpy as jnp
from jax import lax

TILE = 128
TD = 16
NB = 6
GMAX = 4
SWEEPS = 3
CAP = 4
GROUPS = 8
MEMBERS = 4
NTILES = 512
NP = 65536
DEVICES = 32


def draw_particles(key, part):
    subkeys = jax.random.split(jax.random.fold_in(key, 11), 6)
    uniform_draw = jax.random.uniform(subkeys[0], (3, NP), jnp.float32)
    positions = uniform_draw
    masses = jnp.exp(jax.random.uniform(subkeys[1], (1, NP), jnp.float32, math.log(0.5), math.log(2.0))) / (NB * TILE)
    smooth = jax.random.uniform(subkeys[2], (1, NP), jnp.float32, 0.3, 0.5)
    energies = jnp.exp(jax.random.uniform(subkeys[3], (1, NP), jnp.float32, math.log(0.5), math.log(4.0)))
    opacity = jnp.exp(jax.random.uniform(subkeys[4], (1, NP), jnp.float32, math.log(0.05), math.log(20.0)))
    heating = jax.random.uniform(subkeys[5], (1, NP), jnp.float32, 0.0, 1.0)
    return jnp.concatenate([positions, masses, smooth, energies, opacity, heating], axis=0)


def ghost_table(key):
    base_key = jax.random.fold_in(key, 101)
    left_counts = jax.random.randint(jax.random.fold_in(base_key, 1), (DEVICES,), 1, GMAX + 1)
    right_counts = jax.random.randint(jax.random.fold_in(base_key, 2), (DEVICES,), 1, GMAX + 1)
    chosen = jax.random.randint(jax.random.fold_in(base_key, 3), (), 1, DEVICES)
    dev_ids = jnp.arange(DEVICES, dtype=jnp.int32)
    left_counts = jnp.where(dev_ids == chosen, GMAX, left_counts)
    left_counts = jnp.where(dev_ids == 0, 0, left_counts)
    right_counts = jnp.where(dev_ids == DEVICES - 1, 0, right_counts)
    return jnp.stack([left_counts, right_counts], axis=1).astype(jnp.int32)


def draw_ghosts(key, part):
    return ghost_table(key)


def draw_neighbours(key, part):
    table = ghost_table(key)
    tile_ids = jnp.arange(NTILES, dtype=jnp.int32)
    owner_dev = tile_ids // TD
    left_counts = table[owner_dev, 0]
    range_size = left_counts + TD + table[owner_dev, 1]
    itself = left_counts + tile_ids % TD
    others = jax.random.randint(jax.random.fold_in(key, 202), (NTILES, NB - 1), 0, range_size[:, None])
    return jnp.concatenate([itself[:, None], others], axis=1).astype(jnp.int32)


def member_counts(member_key):
    first_key, second_key = jax.random.split(member_key)
    unit_count = GROUPS * CAP
    specials = jnp.array([1 % GROUPS, GROUPS // 2 % GROUPS, (GROUPS - 1) % GROUPS], dtype=jnp.int32)
    keeper = specials[jax.random.randint(first_key, (), 0, 3)]
    unit_ids = jnp.arange(unit_count, dtype=jnp.int32)
    owners = unit_ids // CAP
    is_special = jnp.sum((owners[:, None] == specials[None, :]).astype(jnp.int32), axis=1) > 0
    first_unit = unit_ids % CAP == 0
    boost = jnp.where(owners == keeper, 3 * unit_count, 0) + jnp.where(is_special & first_unit, 2 * unit_count, 0)
    scores = jax.random.permutation(second_key, unit_count).astype(jnp.int32) + boost.astype(jnp.int32)
    ranked = jnp.argsort(-scores, stable=True)
    kept_units = jnp.zeros((unit_count,), jnp.int32).at[ranked[:TD]].set(1)
    return jnp.sum(kept_units.reshape(GROUPS, CAP), axis=1)


def order_of(order_key):
    return jax.random.permutation(order_key, TD).astype(jnp.int32)


def draw_new_slot(key, part):
    base_key = jax.random.fold_in(key, 303)
    counts = jax.vmap(member_counts)(jax.random.split(jax.random.fold_in(base_key, 1), MEMBERS))
    ends = jnp.cumsum(counts, axis=1)
    sender_order = jax.vmap(order_of)(jax.random.split(jax.random.fold_in(base_key, 2), DEVICES))
    receiver_order = jax.vmap(order_of)(jax.random.split(jax.random.fold_in(base_key, 3), DEVICES))
    tile_ids = jnp.arange(NTILES, dtype=jnp.int32)
    owner_dev = tile_ids // TD
    group_of = owner_dev // MEMBERS
    member_of = owner_dev % MEMBERS
    position = sender_order.reshape(-1)
    offset = jnp.sum((ends[member_of] <= position[:, None]).astype(jnp.int32), axis=1)
    dest_group = (group_of + offset) % GROUPS
    dest_dev = dest_group * MEMBERS + member_of
    new_slots = dest_dev * TD + receiver_order[dest_dev, position]
    return new_slots.astype(jnp.int32)


def setup_inputs(seed: int = 0) -> dict:
    key_list = jax.random.split(jax.random.key(seed), 5)
    return {
        "particles": draw_particles(jax.random.fold_in(key_list[4], 71), 0),
        "new_slot": draw_new_slot(jax.random.fold_in(key_list[4], 71), 0),
        "neighbours": draw_neighbours(jax.random.fold_in(key_list[4], 71), 0),
        "ghosts": draw_ghosts(jax.random.fold_in(key_list[4], 71), 0),
    }


KERNEL_NORM = 21.0 / (16.0 * math.pi)
TIME_STEP = 0.05

def geometry(own_fields, near_fields):
    offsets = near_fields[0:3, :, :, None, :] - own_fields[0:3, :, None, :, None]
    distance = jnp.sqrt(lax.optimization_barrier(jnp.sum(offsets * offsets, axis=0)))
    return (offsets, distance)

def pair_forces(own_fields, near_fields, distance):
    mean_smooth = 0.5 * (own_fields[4][:, None, :, None] + near_fields[4][:, :, None, :])
    falloff = jax.nn.relu(1.0 - 0.5 * distance / mean_smooth)
    return 5.0 * KERNEL_NORM * falloff ** 3 / mean_smooth ** 5

def density_kernel(own_items, near_items):
    own_fields = own_items[0]
    near_fields = near_items[0]
    offsets, distance = geometry(own_fields, near_fields)
    smooth = own_fields[4][:, None, :, None]
    scaled = distance / smooth
    falloff = jax.nn.relu(1.0 - 0.5 * scaled)
    weight = KERNEL_NORM * falloff ** 4 * (2.0 * scaled + 1.0) / smooth ** 3
    return lax.optimization_barrier(jnp.sum(near_fields[3][:, :, None, :] * weight, axis=(1, 3)))

def limiter_kernel(own_items, near_items):
    own_fields, own_density, own_energy = own_items
    near_fields, near_density, near_energy = near_items
    offsets, distance = geometry(own_fields, near_fields)
    forces = pair_forces(own_fields, near_fields, distance)
    volume = near_fields[3] / near_density[0]
    change = near_energy[0][:, :, None, :] - own_energy[0][:, None, :, None]
    scaled = volume[:, :, None, :] * forces * change
    gradient = lax.optimization_barrier(jnp.sum(scaled[None] * offsets, axis=(2, 4)))
    stream_ratio = jnp.sqrt(lax.optimization_barrier(jnp.sum(gradient * gradient, axis=0))) / (own_fields[6] * own_density[0] * own_energy[0])
    limiter = (2.0 + stream_ratio) / (6.0 + 3.0 * stream_ratio + stream_ratio * stream_ratio)
    return limiter / (own_fields[6] * own_density[0])

def jacobi_kernel(own_items, near_items):
    own_fields, own_density, own_diffusion = own_items
    near_fields, near_density, near_diffusion, near_energy = near_items
    offsets, distance = geometry(own_fields, near_fields)
    forces = pair_forces(own_fields, near_fields, distance)
    coupling = near_fields[3][:, :, None, :] * (own_diffusion[0][:, None, :, None] + near_diffusion[0][:, :, None, :]) * forces
    coupling = coupling / (own_density[0][:, None, :, None] * near_density[0][:, :, None, :])
    rate_sum = lax.optimization_barrier(jnp.sum(coupling, axis=(1, 3)))
    inflow = lax.optimization_barrier(jnp.sum(coupling * near_energy[0][:, :, None, :], axis=(1, 3)))
    return (own_fields[5] + TIME_STEP * own_fields[7] + TIME_STEP * inflow) / (1.0 + TIME_STEP * rate_sum)

def per_segment(kernel, own_items, all_items, near_index):

    def one_block(dev_id):
        first_tile = dev_id * TD
        own_part = tuple((lax.dynamic_slice_in_dim(values, first_tile, TD, 1) for values in own_items))
        near_rows = lax.dynamic_slice_in_dim(near_index, first_tile, TD, 0)
        near_part = tuple((jnp.take(values, near_rows, axis=1) for values in all_items))
        return kernel(own_part, near_part)
    blocks = lax.map(one_block, jnp.arange(DEVICES, dtype=jnp.int32))
    return blocks.reshape(1, NTILES, TILE)

def reference(particles, new_slot, neighbours, ghosts):
    tiled = particles.reshape(8, NTILES, TILE)
    arranged = jnp.zeros_like(tiled).at[:, new_slot, :].set(tiled)
    device = jnp.arange(NTILES, dtype=jnp.int32) // TD
    near_index = (device * TD - ghosts[device, 0])[:, None] + neighbours
    statics = arranged[0:6]
    density = per_segment(density_kernel, (arranged,), (statics,), near_index)
    energy = arranged[5:6]
    for sweep_step in range(SWEEPS):
        diffusion = per_segment(limiter_kernel, (arranged, density, energy), (statics, density, energy), near_index)
        energy = per_segment(jacobi_kernel, (arranged, density, diffusion), (statics, density, diffusion, energy), near_index)
    return (energy.reshape(-1), density.reshape(-1))
```

```python
import functools
import math

import jax
import jax.numpy as jnp
from jax import lax
from jax.experimental import pallas as pl
from jax.experimental.pallas import tpu as pltpu
from jax.sharding import PartitionSpec as P

TILE = 128
GMAX = 4
SWEEPS = 3
CHUNK = 32
KERNEL_NORM = 21.0 / (16.0 * math.pi)
FORCE_NORM = 5.0 * KERNEL_NORM * 32.0
TIME_STEP = 0.05
SHIFT_E = 2.25
SHIFT_X = 0.5
MESH = pl.DeviceIdType.MESH
F32 = jnp.float32
BF16 = jnp.bfloat16


def row(value, count=8):
    return jnp.broadcast_to(value, (count, TILE))


def split_rows(value):
    high = value.astype(BF16)
    low = (value - high.astype(F32)).astype(BF16)
    return jnp.concatenate([high, low], axis=0)


def kernel(
    groups, members, tc, nb, cap,
    part_ref, slot_ref, near_ref, ghost_ref, energy_ref, density_ref,
    send_buf, recv_buf, ext, cols, force, acc_ref, dens, vol, gv, en, diff, lim, jac, sums,
    a2a_send, a2a_recv, halo_send, halo_recv,
):
    my_group = lax.axis_index("group")
    my_member = lax.axis_index("member")
    me = my_group * members + my_member
    count = groups * members
    has_left = me > 0
    has_right = me < count - 1
    left = lax.rem(me + count - 1, count)
    right = lax.rem(me + 1, count)
    left_id = (left // members, lax.rem(left, members))
    right_id = (right // members, lax.rem(right, members))
    edge = GMAX
    total = tc + 2 * edge

    barrier = pltpu.get_barrier_semaphore()

    def greet(offset, carry):
        target = lax.rem(my_group + offset, groups)
        pl.semaphore_signal(barrier, inc=1, device_id=(target, my_member), device_id_type=MESH)
        return carry

    lax.fori_loop(1, groups, greet, 0)
    for device in (left_id, right_id):
        pl.semaphore_signal(barrier, inc=1, device_id=device, device_id_type=MESH)

    targets = [slot_ref[t] // (tc * members) for t in range(tc)]
    places = []
    for t in range(tc):
        order = jnp.int32(0)
        for u in range(t):
            order = order + jnp.where(targets[u] == targets[t], 1, 0)
        places.append(targets[t] * cap + order)
    labels = [lax.rem(slot_ref[t], tc) + 1 for t in range(tc)]
    place_rows = [jnp.full((8, TILE), p, jnp.int32) for p in places]
    label_rows = [jnp.full((8, TILE), p, jnp.int32).astype(F32) for p in labels]

    def pack(group, carry):
        for c in range(cap):
            bucket = group * cap + c
            tile = jnp.zeros((8, TILE), F32)
            label = jnp.zeros((8, TILE), F32)
            for t in range(tc):
                mask = place_rows[t] == bucket
                tile = jnp.where(mask, part_ref[:, t * TILE : (t + 1) * TILE], tile)
                label = jnp.where(mask, label_rows[t], label)
            send_buf[group, c] = tile
            send_buf[group, cap, c : c + 1, :] = label[0:1]
        return carry

    lax.fori_loop(0, groups, pack, 0)
    pl.semaphore_wait(barrier, groups + 1)

    def a2a_copy(offset):
        target = lax.rem(my_group + offset, groups)
        return pltpu.make_async_remote_copy(
            src_ref=send_buf.at[target],
            dst_ref=recv_buf.at[my_group],
            send_sem=a2a_send.at[offset],
            recv_sem=a2a_recv.at[offset],
            device_id=(target, my_member),
            device_id_type=MESH,
        )

    def a2a_start(offset, carry):
        a2a_copy(offset).start()
        return carry

    def a2a_wait(offset, carry):
        a2a_copy(offset).wait()
        return carry

    lax.fori_loop(1, groups, a2a_start, 0)
    recv_buf[my_group] = send_buf[my_group]
    lax.fori_loop(1, groups, a2a_wait, 0)

    def choose(group, tiles):
        tiles = list(tiles)
        for c in range(cap):
            tile = recv_buf[group, c]
            label = row(recv_buf[group, cap, c : c + 1, :])
            for k in range(tc):
                tiles[k] = jnp.where(label == float(k + 1), tile, tiles[k])
        return tuple(tiles)

    arranged = lax.fori_loop(
        0, groups, choose, tuple(jnp.zeros((8, TILE), F32) for _ in range(tc))
    )
    for k in range(tc):
        ext[edge + k] = arranged[k]

    def halo_copies(number, ref):
        to_left = pltpu.make_async_remote_copy(
            src_ref=ref.at[pl.ds(edge, edge)],
            dst_ref=ref.at[pl.ds(edge + tc, edge)],
            send_sem=halo_send.at[number, 0],
            recv_sem=halo_recv.at[number, 0],
            device_id=left_id,
            device_id_type=MESH,
        )
        to_right = pltpu.make_async_remote_copy(
            src_ref=ref.at[pl.ds(tc, edge)],
            dst_ref=ref.at[pl.ds(0, edge)],
            send_sem=halo_send.at[number, 1],
            recv_sem=halo_recv.at[number, 1],
            device_id=right_id,
            device_id_type=MESH,
        )
        return to_left, to_right

    def halo_start(number, ref):
        to_left, to_right = halo_copies(number, ref)
        pl.when(has_left)(to_left.start)
        pl.when(has_right)(to_right.start)

    def halo_wait(number, ref):
        to_left, to_right = halo_copies(number, ref)
        pl.when(has_right)(to_left.wait_recv)
        pl.when(has_left)(to_right.wait_recv)

    def halo_done(number, ref):
        to_left, to_right = halo_copies(number, ref)
        pl.when(has_left)(to_left.wait_send)
        pl.when(has_right)(to_right.wait_send)

    base = edge - ghost_ref[0, 0]

    def columns(j):
        turned = jnp.transpose(ext[j])
        for place, field in enumerate((0, 1, 2, 3, 4)):
            cols[j, place] = jnp.broadcast_to(turned[:, field : field + 1], (TILE, TILE))
        return None

    def columns_step(j, carry):
        columns(j)
        return carry

    def pair_block(s, slot, j, acc):
        own = ext[edge + s]
        xi, yi, zi, hi = (own[f : f + 1] for f in (0, 1, 2, 4))
        xi, yi, zi, hi, ih = (row(v) for v in (xi, yi, zi, hi, 0.5 / hi))
        for first in range(0, TILE, CHUNK):
            span = pl.ds(first, CHUNK)
            big = (CHUNK // 8, 8, TILE)
            xb, yb, zb, mb, hb = (cols[j, f, span, :].reshape(big) for f in range(5))
            dx, dy, dz = xb - xi, yb - yi, zb - zi
            square = dx * dx + dy * dy + dz * dz
            r = square * lax.rsqrt(jnp.maximum(square, 1e-30))
            u = hb + hi
            inverse = 1.0 / (u * u)
            a = jnp.maximum(u - r, 0.0) * inverse
            f = (a * a) * (a * inverse)
            f = f.reshape(CHUNK, TILE)
            high = f.astype(BF16)
            low = (f - high.astype(F32)).astype(BF16)
            force[s * nb + slot, span, 0:TILE] = high
            force[s * nb + slot, span, TILE : 2 * TILE] = low
            t = jnp.maximum(1.0 - r * ih, 0.0)
            t2 = t * t
            w = (mb * (5.0 - 4.0 * t)) * (t2 * t2)
            acc = acc + jnp.sum(w, axis=0)
        return acc

    halo_start(0, ext)
    lax.fori_loop(edge, edge + tc, columns_step, 0)

    def self_step(s, carry):
        acc_ref[s] = pair_block(s, 0, edge + s, jnp.zeros((8, TILE), F32))
        return carry

    lax.fori_loop(0, tc, self_step, 0)
    halo_wait(0, ext)
    lax.fori_loop(0, edge, columns_step, 0)
    lax.fori_loop(edge + tc, total, columns_step, 0)

    def density_tile(s):
        def other(n, acc):
            return pair_block(s, n, near_ref[s, n] + base, acc)

        acc = lax.fori_loop(1, nb, other, acc_ref[s])
        h = ext[edge + s, 4:5, :]
        value = jnp.sum(acc, axis=0, keepdims=True) * (KERNEL_NORM / (h * h * h))
        dens[edge + s] = value
        density_ref[pl.ds(s, 1), :] = value

    def edge_tile(q):
        return q + (tc - 2 * edge) * (q // edge)

    def density_edge(q, carry):
        density_tile(edge_tile(q))
        return carry

    def density_mid(q, carry):
        density_tile(q)
        return carry

    lax.fori_loop(0, 2 * edge, density_edge, 0)
    halo_start(1, dens)
    lax.fori_loop(edge, tc - edge, density_mid, 0)

    rows = lax.broadcasted_iota(jnp.int32, (8, TILE), 0)
    top = rows < 4

    def limiter_rows(sweep, j):
        lim[j] = split_rows(gv[j] * jnp.where(top, row(en[sweep, j]), 1.0))

    def start_tile(j):
        own = ext[j]
        one_x = jnp.where(lax.rem(rows, 4) == 0, 1.0, pltpu.roll(own, 1, 0) - SHIFT_X)
        two = jnp.where(top, one_x, pltpu.roll(one_x, 4, 0))
        volume = FORCE_NORM * own[3:4] / dens[j]
        vol[j] = volume
        gv[j] = two * row(volume)
        en[0, j] = own[5:6] - SHIFT_E
        limiter_rows(0, j)

    def jacobi_rows(sweep, j):
        vd = row(vol[j] * diff[sweep, j])
        pick = jnp.where(rows == 0, row(en[sweep, j]), jnp.where(rows == 1, 1.0, 0.0))
        jac[j] = split_rows(vd * pick)

    def start_step(j, carry):
        start_tile(j)
        return carry

    def product(table, s):
        parts = [table[edge + s]] + [table[near_ref[s, n] + base] for n in range(1, nb)]
        left_side = jnp.concatenate(parts, axis=1)
        right_side = force[pl.ds(s * nb, nb)].reshape(nb * TILE, 2 * TILE)
        out = jnp.dot(left_side, right_side, preferred_element_type=F32)
        return (out[0:8, 0:TILE] + out[0:8, TILE:]) + (out[8:16, 0:TILE] + out[8:16, TILE:])

    def limiter_tile(sweep, s):
        value = product(lim, s)
        sums[s] = value
        e = en[sweep, edge + s]
        own = ext[edge + s]
        lead = value[0:1] - e * value[4:5]
        square = jnp.zeros((1, TILE), F32)
        for axis in range(3):
            g = value[1 + axis : 2 + axis] - e * value[5 + axis : 6 + axis]
            g = g - (own[axis : axis + 1] - SHIFT_X) * lead
            square = square + g * g
        opaque = own[6:7] * dens[edge + s]
        ratio = jnp.sqrt(square) / (opaque * (e + SHIFT_E))
        diff[sweep, edge + s] = (2.0 + ratio) / ((6.0 + 3.0 * ratio + ratio * ratio) * opaque)
        jacobi_rows(sweep, edge + s)

    def jacobi_tile(sweep, s):
        value = product(jac, s)
        own = ext[edge + s]
        old = sums[s]
        d = diff[sweep, edge + s]
        scale = TIME_STEP / dens[edge + s]
        inflow = d * old[0:1] + value[0:1]
        rate = d * old[4:5] + value[1:2]
        e = (own[5:6] - SHIFT_E + TIME_STEP * own[7:8] + scale * inflow) / (1.0 + scale * rate)
        if sweep == SWEEPS - 1:
            energy_ref[pl.ds(s, 1), :] = e + SHIFT_E
        else:
            en[sweep + 1, edge + s] = e
            limiter_rows(sweep + 1, edge + s)

    def four(work, first):
        for k in range(edge):
            work(first + k)

    def edges(work):
        lax.fori_loop(0, 2, lambda q, c: (four(work, q * (tc - edge)), c)[1], 0)

    def middle(work):
        lax.fori_loop(1, tc // edge - 1, lambda q, c: (four(work, q * edge), c)[1], 0)

    def ghosts(work):
        for j in range(edge):
            work(j)
            work(edge + tc + j)

    lax.fori_loop(edge, edge + tc, start_step, 0)
    halo_wait(1, dens)
    ghosts(start_tile)

    for sweep in range(SWEEPS):
        if sweep > 0:
            halo_wait(2 * sweep + 1, en.at[sweep])
            ghosts(functools.partial(limiter_rows, sweep))
        work = functools.partial(limiter_tile, sweep)
        edges(work)
        halo_start(2 * sweep + 2, diff.at[sweep])
        middle(work)
        halo_wait(2 * sweep + 2, diff.at[sweep])
        ghosts(functools.partial(jacobi_rows, sweep))
        work = functools.partial(jacobi_tile, sweep)
        edges(work)
        if sweep < SWEEPS - 1:
            halo_start(2 * sweep + 3, en.at[sweep + 1])
        middle(work)

    halo_done(0, ext)
    halo_done(1, dens)
    for sweep in range(SWEEPS):
        halo_done(2 * sweep + 2, diff.at[sweep])
        if sweep < SWEEPS - 1:
            halo_done(2 * sweep + 3, en.at[sweep + 1])


def solution(mesh):
    groups, members = mesh.shape["group"], mesh.shape["member"]

    def local(particles, new_slot, neighbours, ghosts):
        tc = new_slot.shape[0]
        nb = neighbours.shape[1]
        cap = max(2, (2 * tc + groups - 1) // groups)
        total = tc + 2 * GMAX
        halos = 2 + 2 * SWEEPS - 1
        vmem = pl.BlockSpec(memory_space=pltpu.VMEM)
        smem = pl.BlockSpec(memory_space=pltpu.SMEM)
        energy, density = pl.pallas_call(
            functools.partial(kernel, groups, members, tc, nb, cap),
            out_shape=[jax.ShapeDtypeStruct((tc, TILE), F32)] * 2,
            in_specs=[vmem, smem, smem, smem],
            out_specs=[vmem, vmem],
            scratch_shapes=[
                pltpu.VMEM((groups, cap + 1, 8, TILE), F32),
                pltpu.VMEM((groups, cap + 1, 8, TILE), F32),
                pltpu.VMEM((total, 8, TILE), F32),
                pltpu.VMEM((total, 5, TILE, TILE), F32),
                pltpu.VMEM((tc * nb, TILE, 2 * TILE), BF16),
                pltpu.VMEM((tc, 8, TILE), F32),
                pltpu.VMEM((total, 1, TILE), F32),
                pltpu.VMEM((total, 1, TILE), F32),
                pltpu.VMEM((total, 8, TILE), F32),
                pltpu.VMEM((SWEEPS, total, 1, TILE), F32),
                pltpu.VMEM((SWEEPS, total, 1, TILE), F32),
                pltpu.VMEM((total, 16, TILE), BF16),
                pltpu.VMEM((total, 16, TILE), BF16),
                pltpu.VMEM((tc, 8, TILE), F32),
                pltpu.SemaphoreType.DMA((groups,)),
                pltpu.SemaphoreType.DMA((groups,)),
                pltpu.SemaphoreType.DMA((halos, 2)),
                pltpu.SemaphoreType.DMA((halos, 2)),
            ],
            compiler_params=pltpu.CompilerParams(
                collective_id=0, has_side_effects=True, vmem_limit_bytes=60 * 1024 * 1024
            ),
        )(particles, new_slot, neighbours, ghosts)
        return energy.reshape(-1), density.reshape(-1)

    in_specs = (
        P(None, ("group", "member")),
        P(("group", "member")),
        P(("group", "member"), None),
        P(("group", "member"), None),
    )
    out_specs = (P(("group", "member")), P(("group", "member")))
    return jax.shard_map(local, mesh=mesh, in_specs=in_specs, out_specs=out_specs, check_vma=False)
```

```python
import functools
import math

import jax
import jax.numpy as jnp
from jax import lax
from jax.experimental import pallas as pl
from jax.experimental.pallas import tpu as pltpu
from jax.sharding import PartitionSpec as P

TILE = 128
GMAX = 4
SWEEPS = 3
CHUNK = 32
KERNEL_NORM = 21.0 / (16.0 * math.pi)
FORCE_NORM = 5.0 * KERNEL_NORM * 32.0
TIME_STEP = 0.05
SHIFT_E = 2.25
SHIFT_X = 0.5
MESH = pl.DeviceIdType.MESH
F32 = jnp.float32
BF16 = jnp.bfloat16


def row(value, count=8):
    return jnp.broadcast_to(value, (count, TILE))


def split_rows(value):
    high = value.astype(BF16)
    low = (value - high.astype(F32)).astype(BF16)
    return jnp.concatenate([high, low], axis=0)


def kernel(
    groups, members, tc, nb, cap,
    part_ref, slot_ref, near_ref, ghost_ref, energy_ref, density_ref,
    send_buf, recv_buf, ext, cols, force, acc_ref, dens, vol, gv, en, diff, lim, jac, sums,
    a2a_send, a2a_recv, halo_send, halo_recv,
):
    my_group = lax.axis_index("group")
    my_member = lax.axis_index("member")
    me = my_group * members + my_member
    count = groups * members
    has_left = me > 0
    has_right = me < count - 1
    left = lax.rem(me + count - 1, count)
    right = lax.rem(me + 1, count)
    left_id = (left // members, lax.rem(left, members))
    right_id = (right // members, lax.rem(right, members))
    edge = GMAX
    total = tc + 2 * edge

    barrier = pltpu.get_barrier_semaphore()

    def greet(offset, carry):
        target = lax.rem(my_group + offset, groups)
        pl.semaphore_signal(barrier, inc=1, device_id=(target, my_member), device_id_type=MESH)
        return carry

    lax.fori_loop(1, groups, greet, 0)
    for device in (left_id, right_id):
        pl.semaphore_signal(barrier, inc=1, device_id=device, device_id_type=MESH)

    targets = [slot_ref[t] // (tc * members) for t in range(tc)]
    places = []
    for t in range(tc):
        order = jnp.int32(0)
        for u in range(t):
            order = order + jnp.where(targets[u] == targets[t], 1, 0)
        places.append(targets[t] * cap + order)
    labels = [lax.rem(slot_ref[t], tc) + 1 for t in range(tc)]
    place_rows = [jnp.full((8, TILE), p, jnp.int32) for p in places]
    label_rows = [jnp.full((8, TILE), p, jnp.int32).astype(F32) for p in labels]

    def pack(group, carry):
        for c in range(cap):
            bucket = group * cap + c
            tile = jnp.zeros((8, TILE), F32)
            label = jnp.zeros((8, TILE), F32)
            for t in range(tc):
                mask = place_rows[t] == bucket
                tile = jnp.where(mask, part_ref[:, t * TILE : (t + 1) * TILE], tile)
                label = jnp.where(mask, label_rows[t], label)
            send_buf[group, c] = tile
            send_buf[group, cap, c : c + 1, :] = label[0:1]
        return carry

    lax.fori_loop(0, groups, pack, 0)
    pl.semaphore_wait(barrier, groups + 1)

    def a2a_copy(offset):
        target = lax.rem(my_group + offset, groups)
        return pltpu.make_async_remote_copy(
            src_ref=send_buf.at[target],
            dst_ref=recv_buf.at[my_group],
            send_sem=a2a_send.at[offset],
            recv_sem=a2a_recv.at[offset],
            device_id=(target, my_member),
            device_id_type=MESH,
        )

    def a2a_start(offset, carry):
        a2a_copy(offset).start()
        return carry

    def a2a_wait(offset, carry):
        a2a_copy(offset).wait()
        return carry

    lax.fori_loop(1, groups, a2a_start, 0)
    recv_buf[my_group] = send_buf[my_group]
    lax.fori_loop(1, groups, a2a_wait, 0)

    def choose(group, tiles):
        tiles = list(tiles)
        for c in range(cap):
            tile = recv_buf[group, c]
            label = row(recv_buf[group, cap, c : c + 1, :])
            for k in range(tc):
                tiles[k] = jnp.where(label == float(k + 1), tile, tiles[k])
        return tuple(tiles)

    arranged = lax.fori_loop(
        0, groups, choose, tuple(jnp.zeros((8, TILE), F32) for _ in range(tc))
    )
    for k in range(tc):
        ext[edge + k] = arranged[k]

    def halo_copies(number, ref):
        to_left = pltpu.make_async_remote_copy(
            src_ref=ref.at[pl.ds(edge, edge)],
            dst_ref=ref.at[pl.ds(edge + tc, edge)],
            send_sem=halo_send.at[number, 0],
            recv_sem=halo_recv.at[number, 0],
            device_id=left_id,
            device_id_type=MESH,
        )
        to_right = pltpu.make_async_remote_copy(
            src_ref=ref.at[pl.ds(tc, edge)],
            dst_ref=ref.at[pl.ds(0, edge)],
            send_sem=halo_send.at[number, 1],
            recv_sem=halo_recv.at[number, 1],
            device_id=right_id,
            device_id_type=MESH,
        )
        return to_left, to_right

    def halo_start(number, ref):
        to_left, to_right = halo_copies(number, ref)
        pl.when(has_left)(to_left.start)
        pl.when(has_right)(to_right.start)

    def halo_wait(number, ref):
        to_left, to_right = halo_copies(number, ref)
        pl.when(has_right)(to_left.wait_recv)
        pl.when(has_left)(to_right.wait_recv)

    def halo_done(number, ref):
        to_left, to_right = halo_copies(number, ref)
        pl.when(has_left)(to_left.wait_send)
        pl.when(has_right)(to_right.wait_send)

    base = edge - ghost_ref[0, 0]

    part_row = lax.broadcasted_iota(jnp.int32, (32, 5 * TILE), 0)
    part_col = lax.broadcasted_iota(jnp.int32, (32, 5 * TILE), 1)
    spread = (
        jnp.where(part_row < 24, 1.0, 0.0)
        * jnp.where(lax.rem(part_row, 8) == part_col // TILE, 1.0, 0.0)
    ).astype(BF16)

    def columns(j):
        fields = ext[j]
        first = fields.astype(BF16).astype(F32)
        rest = fields - first
        second = rest.astype(BF16).astype(F32)
        third = rest - second
        stacked = jnp.concatenate([first, second, third, jnp.zeros((8, TILE), F32)], axis=0)
        turned = jnp.transpose(stacked).astype(BF16)
        wide = jnp.dot(turned, spread, preferred_element_type=F32)
        for place in range(5):
            cols[j, place] = wide[:, place * TILE : (place + 1) * TILE]

    def columns_step(q, carry):
        for k in range(edge):
            columns(q * edge + k)
        return carry

    def pair_block(s, slot, j, acc):
        own = ext[edge + s]
        xi, yi, zi, hi = (own[f : f + 1] for f in (0, 1, 2, 4))
        reach, half = row(2.0 * hi), row(0.5 * hi)
        xi, yi, zi, hi = (row(v) for v in (xi, yi, zi, hi))
        for first in range(0, TILE, CHUNK):
            span = pl.ds(first, CHUNK)
            big = (CHUNK // 8, 8, TILE)
            xb, yb, zb, mb, hb = (cols[j, f, span, :].reshape(big) for f in range(5))
            dx, dy, dz = xb - xi, yb - yi, zb - zi
            square = dx * dx + dy * dy + dz * dz
            r = square * lax.rsqrt(jnp.maximum(square, 1e-30))
            u = hb + hi
            inverse = 1.0 / (u * u)
            a = jnp.maximum(u - r, 0.0) * inverse
            f = (a * a) * (a * inverse)
            f = f.reshape(CHUNK, TILE)
            high = f.astype(BF16)
            low = (f - high.astype(F32)).astype(BF16)
            force[0, s * nb + slot, span, :] = high
            force[1, s * nb + slot, span, :] = low
            t = jnp.maximum(reach - r, 0.0)
            t2 = t * t
            w = (mb * (half + r)) * (t2 * t2)
            acc = acc + jnp.sum(w, axis=0)
        return acc

    halo_start(0, ext)
    lax.fori_loop(1, 1 + tc // edge, columns_step, 0)

    def self_step(s, carry):
        acc_ref[s] = pair_block(s, 0, edge + s, jnp.zeros((8, TILE), F32))
        return carry

    lax.fori_loop(0, tc, self_step, 0)
    halo_wait(0, ext)
    columns_step(0, 0)
    columns_step(1 + tc // edge, 0)

    def density_tile(s):
        def other(n, acc):
            return pair_block(s, n, near_ref[n, s] + base, acc)

        acc = lax.fori_loop(1, nb, other, acc_ref[s])
        h = ext[edge + s, 4:5, :]
        h2 = h * h
        h4 = h2 * h2
        value = jnp.sum(acc, axis=0, keepdims=True) * ((KERNEL_NORM / 8.0) / (h4 * h4))
        dens[edge + s] = value
        density_ref[pl.ds(s, 1), :] = value

    def edge_tile(q):
        return q + (tc - 2 * edge) * (q // edge)

    def density_edge(q, carry):
        density_tile(edge_tile(q))
        return carry

    def density_mid(q, carry):
        density_tile(q)
        return carry

    lax.fori_loop(0, 2 * edge, density_edge, 0)
    halo_start(1, dens)
    lax.fori_loop(edge, tc - edge, density_mid, 0)

    rows = lax.broadcasted_iota(jnp.int32, (8, TILE), 0)
    top = rows < 4

    def limiter_rows(sweep, j):
        lim[j] = split_rows(gv[j] * jnp.where(top, row(en[sweep, j]), 1.0))

    def start_tile(j):
        own = ext[j]
        one_x = jnp.where(lax.rem(rows, 4) == 0, 1.0, pltpu.roll(own, 1, 0) - SHIFT_X)
        two = jnp.where(top, one_x, pltpu.roll(one_x, 4, 0))
        volume = FORCE_NORM * own[3:4] / dens[j]
        vol[j] = volume
        gv[j] = two * row(volume)
        en[0, j] = own[5:6] - SHIFT_E
        limiter_rows(0, j)

    def jacobi_rows(sweep, j):
        vd = row(vol[j] * diff[sweep, j])
        pick = jnp.where(rows == 0, row(en[sweep, j]), jnp.where(rows == 1, 1.0, 0.0))
        jac[j] = split_rows(vd * pick)

    def start_step(j, carry):
        start_tile(j)
        return carry

    def product(table, s):
        parts = [table[edge + s]] + [table[near_ref[n, s] + base] for n in range(1, nb)]
        left_side = jnp.concatenate(parts, axis=1)
        right_side = jnp.concatenate(
            [force[k, pl.ds(s * nb, nb)].reshape(nb * TILE, TILE) for k in range(2)], axis=1
        )
        out = jnp.dot(left_side, right_side, preferred_element_type=F32)
        return (out[0:8, 0:TILE] + out[0:8, TILE:]) + (out[8:16, 0:TILE] + out[8:16, TILE:])

    def limiter_tile(sweep, s):
        value = product(lim, s)
        sums[s] = value
        e = en[sweep, edge + s]
        own = ext[edge + s]
        lead = value[0:1] - e * value[4:5]
        square = jnp.zeros((1, TILE), F32)
        for axis in range(3):
            g = value[1 + axis : 2 + axis] - e * value[5 + axis : 6 + axis]
            g = g - (own[axis : axis + 1] - SHIFT_X) * lead
            square = square + g * g
        opaque = own[6:7] * dens[edge + s]
        ratio = jnp.sqrt(square) / (opaque * (e + SHIFT_E))
        diff[sweep, edge + s] = (2.0 + ratio) / ((6.0 + 3.0 * ratio + ratio * ratio) * opaque)
        jacobi_rows(sweep, edge + s)

    def jacobi_tile(sweep, s):
        value = product(jac, s)
        own = ext[edge + s]
        old = sums[s]
        d = diff[sweep, edge + s]
        scale = TIME_STEP / dens[edge + s]
        inflow = d * old[0:1] + value[0:1]
        rate = d * old[4:5] + value[1:2]
        e = (own[5:6] - SHIFT_E + TIME_STEP * own[7:8] + scale * inflow) / (1.0 + scale * rate)
        if sweep == SWEEPS - 1:
            energy_ref[pl.ds(s, 1), :] = e + SHIFT_E
        else:
            en[sweep + 1, edge + s] = e
            limiter_rows(sweep + 1, edge + s)

    def four(work, first):
        for k in range(edge):
            work(first + k)

    def edges(work):
        lax.fori_loop(0, 2, lambda q, c: (four(work, q * (tc - edge)), c)[1], 0)

    def middle(work):
        lax.fori_loop(1, tc // edge - 1, lambda q, c: (four(work, q * edge), c)[1], 0)

    def ghosts(work):
        for j in range(edge):
            work(j)
            work(edge + tc + j)

    lax.fori_loop(edge, edge + tc, start_step, 0)
    halo_wait(1, dens)
    ghosts(start_tile)

    for sweep in range(SWEEPS):
        if sweep > 0:
            halo_wait(2 * sweep + 1, en.at[sweep])
            ghosts(functools.partial(limiter_rows, sweep))
        work = functools.partial(limiter_tile, sweep)
        edges(work)
        halo_start(2 * sweep + 2, diff.at[sweep])
        middle(work)
        halo_wait(2 * sweep + 2, diff.at[sweep])
        ghosts(functools.partial(jacobi_rows, sweep))
        work = functools.partial(jacobi_tile, sweep)
        edges(work)
        if sweep < SWEEPS - 1:
            halo_start(2 * sweep + 3, en.at[sweep + 1])
        middle(work)

    halo_done(0, ext)
    halo_done(1, dens)
    for sweep in range(SWEEPS):
        halo_done(2 * sweep + 2, diff.at[sweep])
        if sweep < SWEEPS - 1:
            halo_done(2 * sweep + 3, en.at[sweep + 1])


def solution(mesh):
    groups, members = mesh.shape["group"], mesh.shape["member"]

    def local(particles, new_slot, neighbours, ghosts):
        tc = new_slot.shape[0]
        nb = neighbours.shape[1]
        cap = max(2, (2 * tc + groups - 1) // groups)
        total = tc + 2 * GMAX
        halos = 2 + 2 * SWEEPS - 1
        vmem = pl.BlockSpec(memory_space=pltpu.VMEM)
        smem = pl.BlockSpec(memory_space=pltpu.SMEM)
        energy, density = pl.pallas_call(
            functools.partial(kernel, groups, members, tc, nb, cap),
            out_shape=[jax.ShapeDtypeStruct((tc, TILE), F32)] * 2,
            in_specs=[vmem, smem, smem, smem],
            out_specs=[vmem, vmem],
            scratch_shapes=[
                pltpu.VMEM((groups, cap + 1, 8, TILE), F32),
                pltpu.VMEM((groups, cap + 1, 8, TILE), F32),
                pltpu.VMEM((total, 8, TILE), F32),
                pltpu.VMEM((total, 5, TILE, TILE), F32),
                pltpu.VMEM((2, tc * nb, TILE, TILE), BF16),
                pltpu.VMEM((tc, 8, TILE), F32),
                pltpu.VMEM((total, 1, TILE), F32),
                pltpu.VMEM((total, 1, TILE), F32),
                pltpu.VMEM((total, 8, TILE), F32),
                pltpu.VMEM((SWEEPS, total, 1, TILE), F32),
                pltpu.VMEM((SWEEPS, total, 1, TILE), F32),
                pltpu.VMEM((total, 16, TILE), BF16),
                pltpu.VMEM((total, 16, TILE), BF16),
                pltpu.VMEM((tc, 8, TILE), F32),
                pltpu.SemaphoreType.DMA((groups,)),
                pltpu.SemaphoreType.DMA((groups,)),
                pltpu.SemaphoreType.DMA((halos, 2)),
                pltpu.SemaphoreType.DMA((halos, 2)),
            ],
            compiler_params=pltpu.CompilerParams(
                collective_id=0, has_side_effects=True, vmem_limit_bytes=60 * 1024 * 1024
            ),
        )(particles, new_slot, neighbours.T, ghosts)
        return energy.reshape(-1), density.reshape(-1)

    in_specs = (
        P(None, ("group", "member")),
        P(("group", "member")),
        P(("group", "member"), None),
        P(("group", "member"), None),
    )
    out_specs = (P(("group", "member")), P(("group", "member")))
    return jax.shard_map(local, mesh=mesh, in_specs=in_specs, out_specs=out_specs, check_vma=False)
```

```python
import functools
import math

import jax
import jax.numpy as jnp
from jax import lax
from jax.experimental import pallas as pl
from jax.experimental.pallas import tpu as pltpu
from jax.sharding import PartitionSpec as P

TILE = 128
GMAX = 4
SWEEPS = 3
CHUNK = 32
KERNEL_NORM = 21.0 / (16.0 * math.pi)
FORCE_NORM = 5.0 * KERNEL_NORM * 32.0
TIME_STEP = 0.05
SHIFT_E = 2.25
SHIFT_X = 0.5
MESH = pl.DeviceIdType.MESH
F32 = jnp.float32
BF16 = jnp.bfloat16


def row(value, count=8):
    return jnp.broadcast_to(value, (count, TILE))


def split_rows(value):
    high = value.astype(BF16)
    low = (value - high.astype(F32)).astype(BF16)
    return jnp.concatenate([high, low], axis=0)


def kernel(
    groups, members, tc, nb, cap,
    part_ref, slot_ref, near_ref, ghost_ref, energy_ref, density_ref,
    send_buf, recv_buf, ext, cols, force, acc_ref, dens, vol, gv, en, diff, lim, jac, sums,
    a2a_send, a2a_recv, halo_send, halo_recv,
):
    my_group = lax.axis_index("group")
    my_member = lax.axis_index("member")
    me = my_group * members + my_member
    count = groups * members
    has_left = me > 0
    has_right = me < count - 1
    left = lax.rem(me + count - 1, count)
    right = lax.rem(me + 1, count)
    left_id = (left // members, lax.rem(left, members))
    right_id = (right // members, lax.rem(right, members))
    edge = GMAX
    total = tc + 2 * edge

    barrier = pltpu.get_barrier_semaphore()

    def greet(offset, carry):
        target = lax.rem(my_group + offset, groups)
        pl.semaphore_signal(barrier, inc=1, device_id=(target, my_member), device_id_type=MESH)
        return carry

    lax.fori_loop(1, groups, greet, 0)
    for device in (left_id, right_id):
        pl.semaphore_signal(barrier, inc=1, device_id=device, device_id_type=MESH)

    targets = [slot_ref[t] // (tc * members) for t in range(tc)]
    places = []
    for t in range(tc):
        order = jnp.int32(0)
        for u in range(t):
            order = order + jnp.where(targets[u] == targets[t], 1, 0)
        places.append(targets[t] * cap + order)
    labels = [lax.rem(slot_ref[t], tc) + 1 for t in range(tc)]
    place_rows = [jnp.full((8, TILE), p, jnp.int32) for p in places]
    label_rows = [jnp.full((8, TILE), p, jnp.int32).astype(F32) for p in labels]

    def pack(group, carry):
        for c in range(cap):
            bucket = group * cap + c
            tile = jnp.zeros((8, TILE), F32)
            label = jnp.zeros((8, TILE), F32)
            for t in range(tc):
                mask = place_rows[t] == bucket
                tile = jnp.where(mask, part_ref[:, t * TILE : (t + 1) * TILE], tile)
                label = jnp.where(mask, label_rows[t], label)
            send_buf[group, c] = tile
            send_buf[group, cap, c : c + 1, :] = label[0:1]
        return carry

    lax.fori_loop(0, groups, pack, 0)
    pl.semaphore_wait(barrier, groups + 1)

    def a2a_copy(offset):
        target = lax.rem(my_group + offset, groups)
        return pltpu.make_async_remote_copy(
            src_ref=send_buf.at[target],
            dst_ref=recv_buf.at[my_group],
            send_sem=a2a_send.at[offset],
            recv_sem=a2a_recv.at[offset],
            device_id=(target, my_member),
            device_id_type=MESH,
        )

    def a2a_start(offset, carry):
        a2a_copy(offset).start()
        return carry

    def a2a_wait(offset, carry):
        a2a_copy(offset).wait()
        return carry

    lax.fori_loop(1, groups, a2a_start, 0)
    recv_buf[my_group] = send_buf[my_group]
    lax.fori_loop(1, groups, a2a_wait, 0)

    def choose(group, tiles):
        tiles = list(tiles)
        for c in range(cap):
            tile = recv_buf[group, c]
            label = row(recv_buf[group, cap, c : c + 1, :])
            for k in range(tc):
                tiles[k] = jnp.where(label == float(k + 1), tile, tiles[k])
        return tuple(tiles)

    arranged = lax.fori_loop(
        0, groups, choose, tuple(jnp.zeros((8, TILE), F32) for _ in range(tc))
    )
    for k in range(tc):
        ext[edge + k] = arranged[k]

    def halo_copies(number, ref):
        to_left = pltpu.make_async_remote_copy(
            src_ref=ref.at[pl.ds(edge, edge)],
            dst_ref=ref.at[pl.ds(edge + tc, edge)],
            send_sem=halo_send.at[number, 0],
            recv_sem=halo_recv.at[number, 0],
            device_id=left_id,
            device_id_type=MESH,
        )
        to_right = pltpu.make_async_remote_copy(
            src_ref=ref.at[pl.ds(tc, edge)],
            dst_ref=ref.at[pl.ds(0, edge)],
            send_sem=halo_send.at[number, 1],
            recv_sem=halo_recv.at[number, 1],
            device_id=right_id,
            device_id_type=MESH,
        )
        return to_left, to_right

    def halo_start(number, ref):
        to_left, to_right = halo_copies(number, ref)
        pl.when(has_left)(to_left.start)
        pl.when(has_right)(to_right.start)

    def halo_wait(number, ref):
        to_left, to_right = halo_copies(number, ref)
        pl.when(has_right)(to_left.wait_recv)
        pl.when(has_left)(to_right.wait_recv)

    def halo_done(number, ref):
        to_left, to_right = halo_copies(number, ref)
        pl.when(has_left)(to_left.wait_send)
        pl.when(has_right)(to_right.wait_send)

    base = edge - ghost_ref[0, 0]

    part_row = lax.broadcasted_iota(jnp.int32, (32, 5 * TILE), 0)
    part_col = lax.broadcasted_iota(jnp.int32, (32, 5 * TILE), 1)
    spread = (
        jnp.where(part_row < 24, 1.0, 0.0)
        * jnp.where(lax.rem(part_row, 8) == part_col // TILE, 1.0, 0.0)
    ).astype(BF16)

    def columns(j):
        fields = ext[j]
        first = fields.astype(BF16).astype(F32)
        rest = fields - first
        second = rest.astype(BF16).astype(F32)
        third = rest - second
        stacked = jnp.concatenate([first, second, third, jnp.zeros((8, TILE), F32)], axis=0)
        turned = jnp.transpose(stacked).astype(BF16)
        wide = jnp.dot(turned, spread, preferred_element_type=F32)
        for place in range(5):
            cols[j, place] = wide[:, place * TILE : (place + 1) * TILE]

    def columns_step(q, carry):
        for k in range(edge):
            columns(q * edge + k)
        return carry

    def pair_block(s, slot, j, acc):
        own = ext[edge + s]
        xi, yi, zi, hi = (own[f : f + 1] for f in (0, 1, 2, 4))
        reach, half = row(2.0 * hi), row(0.5 * hi)
        xi, yi, zi, hi = (row(v) for v in (xi, yi, zi, hi))
        for first in range(0, TILE, CHUNK):
            span = pl.ds(first, CHUNK)
            big = (CHUNK // 8, 8, TILE)
            xb, yb, zb, mb, hb = (cols[j, f, span, :].reshape(big) for f in range(5))
            dx, dy, dz = xb - xi, yb - yi, zb - zi
            square = dx * dx + dy * dy + dz * dz
            r = square * lax.rsqrt(jnp.maximum(square, 1e-30))
            u = hb + hi
            inverse = 1.0 / (u * u)
            a = jnp.maximum(u - r, 0.0) * inverse
            f = (a * a) * (a * inverse)
            f = f.reshape(CHUNK, TILE)
            high = f.astype(BF16)
            low = (f - high.astype(F32)).astype(BF16)
            force[0, s * nb + slot, span, :] = high
            force[1, s * nb + slot, span, :] = low
            t = jnp.maximum(reach - r, 0.0)
            t2 = t * t
            w = (mb * (half + r)) * (t2 * t2)
            acc = acc + jnp.sum(w, axis=0)
        return acc

    halo_start(0, ext)
    lax.fori_loop(1, 1 + tc // edge, columns_step, 0)

    def self_step(s, carry):
        acc_ref[s] = pair_block(s, 0, edge + s, jnp.zeros((8, TILE), F32))
        return carry

    lax.fori_loop(0, tc, self_step, 0)
    halo_wait(0, ext)
    columns_step(0, 0)
    columns_step(1 + tc // edge, 0)

    def density_tile(s):
        acc = acc_ref[s]
        for n in range(1, nb):
            acc = pair_block(s, n, near_ref[n, s] + base, acc)
        h = ext[edge + s, 4:5, :]
        h2 = h * h
        h4 = h2 * h2
        value = jnp.sum(acc, axis=0, keepdims=True) * ((KERNEL_NORM / 8.0) / (h4 * h4))
        dens[edge + s] = value
        density_ref[pl.ds(s, 1), :] = value

    def edge_tile(q):
        return q + (tc - 2 * edge) * (q // edge)

    def density_edge(q, carry):
        density_tile(edge_tile(q))
        return carry

    def density_mid(q, carry):
        density_tile(q)
        return carry

    lax.fori_loop(0, 2 * edge, density_edge, 0)
    halo_start(1, dens)
    lax.fori_loop(edge, tc - edge, density_mid, 0)

    rows = lax.broadcasted_iota(jnp.int32, (8, TILE), 0)
    top = rows < 4

    def limiter_rows(sweep, j):
        lim[j] = split_rows(gv[j] * jnp.where(top, row(en[sweep, j]), 1.0))

    def start_tile(j):
        own = ext[j]
        one_x = jnp.where(lax.rem(rows, 4) == 0, 1.0, pltpu.roll(own, 1, 0) - SHIFT_X)
        two = jnp.where(top, one_x, pltpu.roll(one_x, 4, 0))
        volume = FORCE_NORM * own[3:4] / dens[j]
        vol[j] = volume
        gv[j] = two * row(volume)
        en[0, j] = own[5:6] - SHIFT_E
        limiter_rows(0, j)

    def jacobi_rows(sweep, j):
        vd = row(vol[j] * diff[sweep, j])
        pick = jnp.where(rows == 0, row(en[sweep, j]), jnp.where(rows == 1, 1.0, 0.0))
        jac[j] = split_rows(vd * pick)

    def start_step(j, carry):
        start_tile(j)
        return carry

    def product(table, s):
        parts = [table[edge + s]] + [table[near_ref[n, s] + base] for n in range(1, nb)]
        left_side = jnp.concatenate(parts, axis=1)
        right_side = jnp.concatenate(
            [force[k, pl.ds(s * nb, nb)].reshape(nb * TILE, TILE) for k in range(2)], axis=1
        )
        out = jnp.dot(left_side, right_side, preferred_element_type=F32)
        return (out[0:8, 0:TILE] + out[0:8, TILE:]) + (out[8:16, 0:TILE] + out[8:16, TILE:])

    def limiter_tile(sweep, s):
        value = product(lim, s)
        sums[s] = value
        e = en[sweep, edge + s]
        own = ext[edge + s]
        lead = value[0:1] - e * value[4:5]
        square = jnp.zeros((1, TILE), F32)
        for axis in range(3):
            g = value[1 + axis : 2 + axis] - e * value[5 + axis : 6 + axis]
            g = g - (own[axis : axis + 1] - SHIFT_X) * lead
            square = square + g * g
        opaque = own[6:7] * dens[edge + s]
        ratio = jnp.sqrt(square) / (opaque * (e + SHIFT_E))
        diff[sweep, edge + s] = (2.0 + ratio) / ((6.0 + 3.0 * ratio + ratio * ratio) * opaque)
        jacobi_rows(sweep, edge + s)

    def jacobi_tile(sweep, s):
        value = product(jac, s)
        own = ext[edge + s]
        old = sums[s]
        d = diff[sweep, edge + s]
        scale = TIME_STEP / dens[edge + s]
        inflow = d * old[0:1] + value[0:1]
        rate = d * old[4:5] + value[1:2]
        e = (own[5:6] - SHIFT_E + TIME_STEP * own[7:8] + scale * inflow) / (1.0 + scale * rate)
        if sweep == SWEEPS - 1:
            energy_ref[pl.ds(s, 1), :] = e + SHIFT_E
        else:
            en[sweep + 1, edge + s] = e
            limiter_rows(sweep + 1, edge + s)

    def edges(work):
        for k in range(edge):
            work(k)
            work(tc - edge + k)

    def middle(work):
        for s in range(edge, tc - edge):
            work(s)

    def ghosts(work):
        for j in range(edge):
            work(j)
            work(edge + tc + j)

    lax.fori_loop(edge, edge + tc, start_step, 0)
    halo_wait(1, dens)
    ghosts(start_tile)

    for sweep in range(SWEEPS):
        if sweep > 0:
            halo_wait(2 * sweep + 1, en.at[sweep])
            ghosts(functools.partial(limiter_rows, sweep))
        work = functools.partial(limiter_tile, sweep)
        edges(work)
        halo_start(2 * sweep + 2, diff.at[sweep])
        middle(work)
        halo_wait(2 * sweep + 2, diff.at[sweep])
        ghosts(functools.partial(jacobi_rows, sweep))
        work = functools.partial(jacobi_tile, sweep)
        edges(work)
        if sweep < SWEEPS - 1:
            halo_start(2 * sweep + 3, en.at[sweep + 1])
        middle(work)

    halo_done(0, ext)
    halo_done(1, dens)
    for sweep in range(SWEEPS):
        halo_done(2 * sweep + 2, diff.at[sweep])
        if sweep < SWEEPS - 1:
            halo_done(2 * sweep + 3, en.at[sweep + 1])


def solution(mesh):
    groups, members = mesh.shape["group"], mesh.shape["member"]

    def local(particles, new_slot, neighbours, ghosts):
        tc = new_slot.shape[0]
        nb = neighbours.shape[1]
        cap = max(2, (2 * tc + groups - 1) // groups)
        total = tc + 2 * GMAX
        halos = 2 + 2 * SWEEPS - 1
        vmem = pl.BlockSpec(memory_space=pltpu.VMEM)
        smem = pl.BlockSpec(memory_space=pltpu.SMEM)
        energy, density = pl.pallas_call(
            functools.partial(kernel, groups, members, tc, nb, cap),
            out_shape=[jax.ShapeDtypeStruct((tc, TILE), F32)] * 2,
            in_specs=[vmem, smem, smem, smem],
            out_specs=[vmem, vmem],
            scratch_shapes=[
                pltpu.VMEM((groups, cap + 1, 8, TILE), F32),
                pltpu.VMEM((groups, cap + 1, 8, TILE), F32),
                pltpu.VMEM((total, 8, TILE), F32),
                pltpu.VMEM((total, 5, TILE, TILE), F32),
                pltpu.VMEM((2, tc * nb, TILE, TILE), BF16),
                pltpu.VMEM((tc, 8, TILE), F32),
                pltpu.VMEM((total, 1, TILE), F32),
                pltpu.VMEM((total, 1, TILE), F32),
                pltpu.VMEM((total, 8, TILE), F32),
                pltpu.VMEM((SWEEPS, total, 1, TILE), F32),
                pltpu.VMEM((SWEEPS, total, 1, TILE), F32),
                pltpu.VMEM((total, 16, TILE), BF16),
                pltpu.VMEM((total, 16, TILE), BF16),
                pltpu.VMEM((tc, 8, TILE), F32),
                pltpu.SemaphoreType.DMA((groups,)),
                pltpu.SemaphoreType.DMA((groups,)),
                pltpu.SemaphoreType.DMA((halos, 2)),
                pltpu.SemaphoreType.DMA((halos, 2)),
            ],
            compiler_params=pltpu.CompilerParams(
                collective_id=0, has_side_effects=True, vmem_limit_bytes=60 * 1024 * 1024
            ),
        )(particles, new_slot, neighbours.T, ghosts)
        return energy.reshape(-1), density.reshape(-1)

    in_specs = (
        P(None, ("group", "member")),
        P(("group", "member")),
        P(("group", "member"), None),
        P(("group", "member"), None),
    )
    out_specs = (P(("group", "member")), P(("group", "member")))
    return jax.shard_map(local, mesh=mesh, in_specs=in_specs, out_specs=out_specs, check_vma=False)
```

```python
import functools
import math

import jax
import jax.numpy as jnp
from jax import lax
from jax.experimental import pallas as pl
from jax.experimental.pallas import tpu as pltpu
from jax.sharding import PartitionSpec as P

TILE = 128
GMAX = 4
SWEEPS = 3
CHUNK = 32
KERNEL_NORM = 21.0 / (16.0 * math.pi)
FORCE_NORM = 5.0 * KERNEL_NORM * 32.0
TIME_STEP = 0.05
SHIFT_E = 2.25
SHIFT_X = 0.5
MESH = pl.DeviceIdType.MESH
F32 = jnp.float32
BF16 = jnp.bfloat16


def row(value, count=8):
    return jnp.broadcast_to(value, (count, TILE))


def split_rows(value):
    high = value.astype(BF16)
    low = (value - high.astype(F32)).astype(BF16)
    return jnp.concatenate([high, low], axis=0)


def kernel(
    groups, members, tc, nb, cap,
    part_ref, slot_ref, near_ref, ghost_ref, energy_ref, density_ref,
    send_buf, recv_buf, ext, cols, force, acc_ref, dens, vol, gv, en, diff, lim, jac, sums, dist,
    a2a_send, a2a_recv, halo_send, halo_recv,
):
    my_group = lax.axis_index("group")
    my_member = lax.axis_index("member")
    me = my_group * members + my_member
    count = groups * members
    has_left = me > 0
    has_right = me < count - 1
    left = lax.rem(me + count - 1, count)
    right = lax.rem(me + 1, count)
    left_id = (left // members, lax.rem(left, members))
    right_id = (right // members, lax.rem(right, members))
    edge = GMAX
    total = tc + 2 * edge

    barrier = pltpu.get_barrier_semaphore()

    def greet(offset, carry):
        target = lax.rem(my_group + offset, groups)
        pl.semaphore_signal(barrier, inc=1, device_id=(target, my_member), device_id_type=MESH)
        return carry

    lax.fori_loop(1, groups, greet, 0)
    for device in (left_id, right_id):
        pl.semaphore_signal(barrier, inc=1, device_id=device, device_id_type=MESH)

    targets = [slot_ref[t] // (tc * members) for t in range(tc)]
    places = []
    for t in range(tc):
        order = jnp.int32(0)
        for u in range(t):
            order = order + jnp.where(targets[u] == targets[t], 1, 0)
        places.append(targets[t] * cap + order)
    labels = [lax.rem(slot_ref[t], tc) + 1 for t in range(tc)]
    place_rows = [jnp.full((8, TILE), p, jnp.int32) for p in places]
    label_rows = [jnp.full((8, TILE), p, jnp.int32).astype(F32) for p in labels]

    def pack(group, carry):
        for c in range(cap):
            bucket = group * cap + c
            tile = jnp.zeros((8, TILE), F32)
            label = jnp.zeros((8, TILE), F32)
            for t in range(tc):
                mask = place_rows[t] == bucket
                tile = jnp.where(mask, part_ref[:, t * TILE : (t + 1) * TILE], tile)
                label = jnp.where(mask, label_rows[t], label)
            send_buf[group, c] = tile
            send_buf[group, cap, c : c + 1, :] = label[0:1]
        return carry

    lax.fori_loop(0, groups, pack, 0)
    pl.semaphore_wait(barrier, groups + 1)

    def a2a_copy(offset):
        target = lax.rem(my_group + offset, groups)
        return pltpu.make_async_remote_copy(
            src_ref=send_buf.at[target],
            dst_ref=recv_buf.at[my_group],
            send_sem=a2a_send.at[offset],
            recv_sem=a2a_recv.at[offset],
            device_id=(target, my_member),
            device_id_type=MESH,
        )

    def a2a_start(offset, carry):
        a2a_copy(offset).start()
        return carry

    def a2a_wait(offset, carry):
        a2a_copy(offset).wait()
        return carry

    lax.fori_loop(1, groups, a2a_start, 0)
    recv_buf[my_group] = send_buf[my_group]
    lax.fori_loop(1, groups, a2a_wait, 0)

    def choose(group, tiles):
        tiles = list(tiles)
        for c in range(cap):
            tile = recv_buf[group, c]
            label = row(recv_buf[group, cap, c : c + 1, :])
            for k in range(tc):
                tiles[k] = jnp.where(label == float(k + 1), tile, tiles[k])
        return tuple(tiles)

    arranged = lax.fori_loop(
        0, groups, choose, tuple(jnp.zeros((8, TILE), F32) for _ in range(tc))
    )
    for k in range(tc):
        ext[edge + k] = arranged[k]

    def halo_copies(number, ref):
        to_left = pltpu.make_async_remote_copy(
            src_ref=ref.at[pl.ds(edge, edge)],
            dst_ref=ref.at[pl.ds(edge + tc, edge)],
            send_sem=halo_send.at[number, 0],
            recv_sem=halo_recv.at[number, 0],
            device_id=left_id,
            device_id_type=MESH,
        )
        to_right = pltpu.make_async_remote_copy(
            src_ref=ref.at[pl.ds(tc, edge)],
            dst_ref=ref.at[pl.ds(0, edge)],
            send_sem=halo_send.at[number, 1],
            recv_sem=halo_recv.at[number, 1],
            device_id=right_id,
            device_id_type=MESH,
        )
        return to_left, to_right

    def halo_start(number, ref):
        to_left, to_right = halo_copies(number, ref)
        pl.when(has_left)(to_left.start)
        pl.when(has_right)(to_right.start)

    def halo_wait(number, ref):
        to_left, to_right = halo_copies(number, ref)
        pl.when(has_right)(to_left.wait_recv)
        pl.when(has_left)(to_right.wait_recv)

    def halo_done(number, ref):
        to_left, to_right = halo_copies(number, ref)
        pl.when(has_left)(to_left.wait_send)
        pl.when(has_right)(to_right.wait_send)

    base = edge - ghost_ref[0, 0]

    part_row = lax.broadcasted_iota(jnp.int32, (32, 5 * TILE), 0)
    part_col = lax.broadcasted_iota(jnp.int32, (32, 5 * TILE), 1)
    spread = (
        jnp.where(part_row < 24, 1.0, 0.0)
        * jnp.where(lax.rem(part_row, 8) == part_col // TILE, 1.0, 0.0)
    ).astype(BF16)

    def columns(j):
        fields = ext[j]
        first = fields.astype(BF16).astype(F32)
        rest = fields - first
        second = rest.astype(BF16).astype(F32)
        third = rest - second
        stacked = jnp.concatenate([first, second, third, jnp.zeros((8, TILE), F32)], axis=0)
        turned = jnp.transpose(stacked).astype(BF16)
        wide = jnp.dot(turned, spread, preferred_element_type=F32)
        for place in range(5):
            cols[j, place] = wide[:, place * TILE : (place + 1) * TILE]

    def columns_step(q, carry):
        for k in range(edge):
            columns(q * edge + k)
        return carry

    def store_force(s, slot, span, r, u):
        inverse = 1.0 / (u * u)
        a = jnp.maximum(u - r, 0.0) * inverse
        f = (a * a) * (a * inverse)
        f = f.reshape(CHUNK, TILE)
        high = f.astype(BF16)
        force[0, s * nb + slot, span, :] = high
        force[1, s * nb + slot, span, :] = (f - high.astype(F32)).astype(BF16)

    def force_block(s, slot, j):
        hi = row(ext[edge + s][4:5])
        for first in range(0, TILE, CHUNK):
            span = pl.ds(first, CHUNK)
            big = (CHUNK // 8, 8, TILE)
            r = dist[(s - edge) * nb + slot, span, :].reshape(big)
            store_force(s, slot, span, r, cols[j, 4, span, :].reshape(big) + hi)

    def pair_block(s, slot, j, acc, keep=False):
        own = ext[edge + s]
        xi, yi, zi, hi = (own[f : f + 1] for f in (0, 1, 2, 4))
        reach, half = row(2.0 * hi), row(0.5 * hi)
        xi, yi, zi, hi = (row(v) for v in (xi, yi, zi, hi))
        for first in range(0, TILE, CHUNK):
            span = pl.ds(first, CHUNK)
            big = (CHUNK // 8, 8, TILE)
            xb, yb, zb, mb, hb = (cols[j, f, span, :].reshape(big) for f in range(5))
            dx, dy, dz = xb - xi, yb - yi, zb - zi
            square = dx * dx + dy * dy + dz * dz
            r = square * lax.rsqrt(jnp.maximum(square, 1e-30))
            if keep:
                dist[(s - edge) * nb + slot, span, :] = r.reshape(CHUNK, TILE)
            else:
                store_force(s, slot, span, r, hb + hi)
            t = jnp.maximum(reach - r, 0.0)
            t2 = t * t
            w = (mb * (half + r)) * (t2 * t2)
            acc = acc + jnp.sum(w, axis=0)
        return acc

    halo_start(0, ext)
    lax.fori_loop(1, 1 + tc // edge, columns_step, 0)

    def self_step(s, carry):
        acc_ref[s] = pair_block(s, 0, edge + s, jnp.zeros((8, TILE), F32))
        return carry

    lax.fori_loop(0, tc, self_step, 0)
    halo_wait(0, ext)
    columns_step(0, 0)
    columns_step(1 + tc // edge, 0)

    def density_tile(s, keep):
        acc = acc_ref[s]
        for n in range(1, nb):
            acc = pair_block(s, n, near_ref[n, s] + base, acc, keep)
        h = ext[edge + s, 4:5, :]
        h2 = h * h
        h4 = h2 * h2
        value = jnp.sum(acc, axis=0, keepdims=True) * ((KERNEL_NORM / 8.0) / (h4 * h4))
        dens[edge + s] = value
        density_ref[pl.ds(s, 1), :] = value

    def edge_tile(q):
        return q + (tc - 2 * edge) * (q // edge)

    def density_edge(q, carry):
        density_tile(edge_tile(q), False)
        return carry

    def density_mid(q, carry):
        density_tile(q, True)
        return carry

    def force_mid(s, carry):
        for n in range(1, nb):
            force_block(s, n, near_ref[n, s] + base)
        return carry

    lax.fori_loop(0, 2 * edge, density_edge, 0)
    halo_start(1, dens)
    lax.fori_loop(edge, tc - edge, density_mid, 0)

    rows = lax.broadcasted_iota(jnp.int32, (8, TILE), 0)
    top = rows < 4

    def limiter_rows(sweep, j):
        lim[j] = split_rows(gv[j] * jnp.where(top, row(en[sweep, j]), 1.0))

    def start_tile(j):
        own = ext[j]
        one_x = jnp.where(lax.rem(rows, 4) == 0, 1.0, pltpu.roll(own, 1, 0) - SHIFT_X)
        two = jnp.where(top, one_x, pltpu.roll(one_x, 4, 0))
        volume = FORCE_NORM * own[3:4] / dens[j]
        vol[j] = volume
        gv[j] = two * row(volume)
        en[0, j] = own[5:6] - SHIFT_E
        limiter_rows(0, j)

    def jacobi_rows(sweep, j):
        vd = row(vol[j] * diff[sweep, j])
        pick = jnp.where(rows == 0, row(en[sweep, j]), jnp.where(rows == 1, 1.0, 0.0))
        jac[j] = split_rows(vd * pick)

    def start_step(j, carry):
        start_tile(j)
        return carry

    def product(table, s):
        parts = [table[edge + s]] + [table[near_ref[n, s] + base] for n in range(1, nb)]
        left_side = jnp.concatenate(parts, axis=1)
        right_side = jnp.concatenate(
            [force[k, pl.ds(s * nb, nb)].reshape(nb * TILE, TILE) for k in range(2)], axis=1
        )
        out = jnp.dot(left_side, right_side, preferred_element_type=F32)
        return (out[0:8, 0:TILE] + out[0:8, TILE:]) + (out[8:16, 0:TILE] + out[8:16, TILE:])

    def limiter_tile(sweep, s):
        value = product(lim, s)
        sums[s] = value
        e = en[sweep, edge + s]
        own = ext[edge + s]
        lead = value[0:1] - e * value[4:5]
        square = jnp.zeros((1, TILE), F32)
        for axis in range(3):
            g = value[1 + axis : 2 + axis] - e * value[5 + axis : 6 + axis]
            g = g - (own[axis : axis + 1] - SHIFT_X) * lead
            square = square + g * g
        opaque = own[6:7] * dens[edge + s]
        ratio = jnp.sqrt(square) / (opaque * (e + SHIFT_E))
        diff[sweep, edge + s] = (2.0 + ratio) / ((6.0 + 3.0 * ratio + ratio * ratio) * opaque)
        jacobi_rows(sweep, edge + s)

    def jacobi_tile(sweep, s):
        value = product(jac, s)
        own = ext[edge + s]
        old = sums[s]
        d = diff[sweep, edge + s]
        scale = TIME_STEP / dens[edge + s]
        inflow = d * old[0:1] + value[0:1]
        rate = d * old[4:5] + value[1:2]
        e = (own[5:6] - SHIFT_E + TIME_STEP * own[7:8] + scale * inflow) / (1.0 + scale * rate)
        if sweep == SWEEPS - 1:
            energy_ref[pl.ds(s, 1), :] = e + SHIFT_E
        else:
            en[sweep + 1, edge + s] = e
            limiter_rows(sweep + 1, edge + s)

    flag = my_member // max(members - 1, 1)

    def edges(work, number=None, ref=None):
        lead = (tc - edge) * flag
        for k in range(edge):
            work(lead + k)
        if ref is not None:
            to_left, to_right = halo_copies(number, ref)
            pl.when(jnp.logical_and(has_left, flag == 0))(to_left.start)
            pl.when(jnp.logical_and(has_right, flag > 0))(to_right.start)
        for k in range(edge):
            work(tc - edge - lead + k)
        if ref is not None:
            pl.when(jnp.logical_and(has_right, flag == 0))(to_right.start)
            pl.when(jnp.logical_and(has_left, flag > 0))(to_left.start)

    def middle(work):
        for s in range(edge, tc - edge):
            work(s)

    def ghosts(work):
        for j in range(edge):
            work(j)
            work(edge + tc + j)

    lax.fori_loop(edge, edge + tc, start_step, 0)
    halo_wait(1, dens)
    ghosts(start_tile)

    for sweep in range(SWEEPS):
        if sweep > 0:
            halo_wait(2 * sweep + 1, en.at[sweep])
            ghosts(functools.partial(limiter_rows, sweep))
        work = functools.partial(limiter_tile, sweep)
        edges(work, 2 * sweep + 2, diff.at[sweep])
        if sweep == 0:
            lax.fori_loop(edge, tc - edge, force_mid, 0)
        middle(work)
        halo_wait(2 * sweep + 2, diff.at[sweep])
        ghosts(functools.partial(jacobi_rows, sweep))
        work = functools.partial(jacobi_tile, sweep)
        if sweep < SWEEPS - 1:
            edges(work, 2 * sweep + 3, en.at[sweep + 1])
        else:
            edges(work)
        middle(work)

    halo_done(0, ext)
    halo_done(1, dens)
    for sweep in range(SWEEPS):
        halo_done(2 * sweep + 2, diff.at[sweep])
        if sweep < SWEEPS - 1:
            halo_done(2 * sweep + 3, en.at[sweep + 1])


def solution(mesh):
    groups, members = mesh.shape["group"], mesh.shape["member"]

    def local(particles, new_slot, neighbours, ghosts):
        tc = new_slot.shape[0]
        nb = neighbours.shape[1]
        cap = max(2, (2 * tc + groups - 1) // groups)
        total = tc + 2 * GMAX
        halos = 2 + 2 * SWEEPS - 1
        vmem = pl.BlockSpec(memory_space=pltpu.VMEM)
        smem = pl.BlockSpec(memory_space=pltpu.SMEM)
        energy, density = pl.pallas_call(
            functools.partial(kernel, groups, members, tc, nb, cap),
            out_shape=[jax.ShapeDtypeStruct((tc, TILE), F32)] * 2,
            in_specs=[vmem, smem, smem, smem],
            out_specs=[vmem, vmem],
            scratch_shapes=[
                pltpu.VMEM((groups, cap + 1, 8, TILE), F32),
                pltpu.VMEM((groups, cap + 1, 8, TILE), F32),
                pltpu.VMEM((total, 8, TILE), F32),
                pltpu.VMEM((total, 5, TILE, TILE), F32),
                pltpu.VMEM((2, tc * nb, TILE, TILE), BF16),
                pltpu.VMEM((tc, 8, TILE), F32),
                pltpu.VMEM((total, 1, TILE), F32),
                pltpu.VMEM((total, 1, TILE), F32),
                pltpu.VMEM((total, 8, TILE), F32),
                pltpu.VMEM((SWEEPS, total, 1, TILE), F32),
                pltpu.VMEM((SWEEPS, total, 1, TILE), F32),
                pltpu.VMEM((total, 16, TILE), BF16),
                pltpu.VMEM((total, 16, TILE), BF16),
                pltpu.VMEM((tc, 8, TILE), F32),
                pltpu.VMEM(((tc - 2 * GMAX) * nb, TILE, TILE), F32),
                pltpu.SemaphoreType.DMA((groups,)),
                pltpu.SemaphoreType.DMA((groups,)),
                pltpu.SemaphoreType.DMA((halos, 2)),
                pltpu.SemaphoreType.DMA((halos, 2)),
            ],
            compiler_params=pltpu.CompilerParams(
                collective_id=0, has_side_effects=True, vmem_limit_bytes=60 * 1024 * 1024
            ),
        )(particles, new_slot, neighbours.T, ghosts)
        return energy.reshape(-1), density.reshape(-1)

    in_specs = (
        P(None, ("group", "member")),
        P(("group", "member")),
        P(("group", "member"), None),
        P(("group", "member"), None),
    )
    out_specs = (P(("group", "member")), P(("group", "member")))
    return jax.shard_map(local, mesh=mesh, in_specs=in_specs, out_specs=out_specs, check_vma=False)
```

```python
import functools
import math

import jax
import jax.numpy as jnp
from jax import lax
from jax.experimental import pallas as pl
from jax.experimental.pallas import tpu as pltpu
from jax.sharding import PartitionSpec as P

TILE = 128
GMAX = 4
SWEEPS = 3
CHUNK = 32
KERNEL_NORM = 21.0 / (16.0 * math.pi)
FORCE_NORM = 5.0 * KERNEL_NORM * 32.0
TIME_STEP = 0.05
SHIFT_E = 2.25
SHIFT_X = 0.5
MESH = pl.DeviceIdType.MESH
F32 = jnp.float32
BF16 = jnp.bfloat16


def row(value, count=8):
    return jnp.broadcast_to(value, (count, TILE))


def split_rows(value):
    high = value.astype(BF16)
    low = (value - high.astype(F32)).astype(BF16)
    return jnp.concatenate([high, low], axis=0)


def kernel(
    groups, members, tc, nb, cap,
    part_ref, slot_ref, near_ref, ghost_ref, out_ref,
    send_buf, recv_buf, ext, cols, force, acc_ref, dens, vol, gv, en, diff, lim, jac, sums, dist,
    a2a_send, a2a_recv, halo_send, halo_recv,
):
    my_group = lax.axis_index("group")
    my_member = lax.axis_index("member")
    me = my_group * members + my_member
    count = groups * members
    has_left = me > 0
    has_right = me < count - 1
    left = lax.rem(me + count - 1, count)
    right = lax.rem(me + 1, count)
    left_id = (left // members, lax.rem(left, members))
    right_id = (right // members, lax.rem(right, members))
    edge = GMAX
    total = tc + 2 * edge

    barrier = pltpu.get_barrier_semaphore()

    def greet(offset, carry):
        target = lax.rem(my_group + offset, groups)
        pl.semaphore_signal(barrier, inc=1, device_id=(target, my_member), device_id_type=MESH)
        return carry

    lax.fori_loop(1, groups, greet, 0)
    for device in (left_id, right_id):
        pl.semaphore_signal(barrier, inc=1, device_id=device, device_id_type=MESH)

    targets = [slot_ref[t] // (tc * members) for t in range(tc)]
    places = []
    for t in range(tc):
        order = jnp.int32(0)
        for u in range(t):
            order = order + jnp.where(targets[u] == targets[t], 1, 0)
        places.append(targets[t] * cap + order)
    labels = [lax.rem(slot_ref[t], tc) + 1 for t in range(tc)]
    place_rows = [jnp.full((8, TILE), p, jnp.int32) for p in places]
    label_rows = [jnp.full((8, TILE), p, jnp.int32).astype(F32) for p in labels]

    def pack(group, carry):
        for c in range(cap):
            bucket = group * cap + c
            tile = jnp.zeros((8, TILE), F32)
            label = jnp.zeros((8, TILE), F32)
            for t in range(tc):
                mask = place_rows[t] == bucket
                tile = jnp.where(mask, part_ref[:, t * TILE : (t + 1) * TILE], tile)
                label = jnp.where(mask, label_rows[t], label)
            send_buf[group, c] = tile
            send_buf[group, cap, c : c + 1, :] = label[0:1]
        return carry

    lax.fori_loop(0, groups, pack, 0)
    pl.semaphore_wait(barrier, groups + 1)

    def a2a_copy(offset):
        target = lax.rem(my_group + offset, groups)
        return pltpu.make_async_remote_copy(
            src_ref=send_buf.at[target],
            dst_ref=recv_buf.at[my_group],
            send_sem=a2a_send.at[offset],
            recv_sem=a2a_recv.at[offset],
            device_id=(target, my_member),
            device_id_type=MESH,
        )

    def a2a_start(offset, carry):
        a2a_copy(offset).start()
        return carry

    def a2a_wait(offset, carry):
        a2a_copy(offset).wait()
        return carry

    lax.fori_loop(1, groups, a2a_start, 0)
    recv_buf[my_group] = send_buf[my_group]
    lax.fori_loop(1, groups, a2a_wait, 0)

    def choose(group, tiles):
        tiles = list(tiles)
        for c in range(cap):
            tile = recv_buf[group, c]
            label = row(recv_buf[group, cap, c : c + 1, :])
            for k in range(tc):
                tiles[k] = jnp.where(label == float(k + 1), tile, tiles[k])
        return tuple(tiles)

    arranged = lax.fori_loop(
        0, groups, choose, tuple(jnp.zeros((8, TILE), F32) for _ in range(tc))
    )
    for k in range(tc):
        ext[edge + k] = arranged[k]

    def halo_copies(number, ref):
        to_left = pltpu.make_async_remote_copy(
            src_ref=ref.at[pl.ds(edge, edge)],
            dst_ref=ref.at[pl.ds(edge + tc, edge)],
            send_sem=halo_send.at[number, 0],
            recv_sem=halo_recv.at[number, 0],
            device_id=left_id,
            device_id_type=MESH,
        )
        to_right = pltpu.make_async_remote_copy(
            src_ref=ref.at[pl.ds(tc, edge)],
            dst_ref=ref.at[pl.ds(0, edge)],
            send_sem=halo_send.at[number, 1],
            recv_sem=halo_recv.at[number, 1],
            device_id=right_id,
            device_id_type=MESH,
        )
        return to_left, to_right

    def halo_start(number, ref):
        to_left, to_right = halo_copies(number, ref)
        pl.when(has_left)(to_left.start)
        pl.when(has_right)(to_right.start)

    def halo_wait(number, ref):
        to_left, to_right = halo_copies(number, ref)
        pl.when(has_right)(to_left.wait_recv)
        pl.when(has_left)(to_right.wait_recv)

    def halo_done(number, ref):
        to_left, to_right = halo_copies(number, ref)
        pl.when(has_left)(to_left.wait_send)
        pl.when(has_right)(to_right.wait_send)

    base = edge - ghost_ref[0, 0]

    part_row = lax.broadcasted_iota(jnp.int32, (32, 5 * TILE), 0)
    part_col = lax.broadcasted_iota(jnp.int32, (32, 5 * TILE), 1)
    spread = (
        jnp.where(part_row < 24, 1.0, 0.0)
        * jnp.where(lax.rem(part_row, 8) == part_col // TILE, 1.0, 0.0)
    ).astype(BF16)

    def columns(j):
        fields = ext[j]
        first = fields.astype(BF16).astype(F32)
        rest = fields - first
        second = rest.astype(BF16).astype(F32)
        third = rest - second
        stacked = jnp.concatenate([first, second, third, jnp.zeros((8, TILE), F32)], axis=0)
        turned = jnp.transpose(stacked).astype(BF16)
        wide = jnp.dot(turned, spread, preferred_element_type=F32)
        for place in range(5):
            cols[j, place] = wide[:, place * TILE : (place + 1) * TILE]

    def columns_step(q, carry):
        for k in range(edge):
            columns(q * edge + k)
        return carry

    def store_force(s, slot, span, r, u):
        inverse = 1.0 / (u * u)
        a = jnp.maximum(u - r, 0.0) * inverse
        f = (a * a) * (a * inverse)
        f = f.reshape(CHUNK, TILE)
        high = f.astype(BF16)
        force[0, s * nb + slot, span, :] = high
        force[1, s * nb + slot, span, :] = (f - high.astype(F32)).astype(BF16)

    def force_block(s, slot, j):
        hi = row(ext[edge + s][4:5])
        for first in range(0, TILE, CHUNK):
            span = pl.ds(first, CHUNK)
            big = (CHUNK // 8, 8, TILE)
            r = dist[(s - edge) * nb + slot, span, :].reshape(big)
            store_force(s, slot, span, r, cols[j, 4, span, :].reshape(big) + hi)

    def pair_block(s, slot, j, acc, keep=False):
        own = ext[edge + s]
        xi, yi, zi, hi = (own[f : f + 1] for f in (0, 1, 2, 4))
        reach, half = row(2.0 * hi), row(0.5 * hi)
        xi, yi, zi, hi = (row(v) for v in (xi, yi, zi, hi))
        for first in range(0, TILE, CHUNK):
            span = pl.ds(first, CHUNK)
            big = (CHUNK // 8, 8, TILE)
            xb, yb, zb, mb, hb = (cols[j, f, span, :].reshape(big) for f in range(5))
            dx, dy, dz = xb - xi, yb - yi, zb - zi
            square = dx * dx + dy * dy + dz * dz
            r = square * lax.rsqrt(jnp.maximum(square, 1e-30))
            if keep:
                dist[(s - edge) * nb + slot, span, :] = r.reshape(CHUNK, TILE)
            else:
                store_force(s, slot, span, r, hb + hi)
            t = jnp.maximum(reach - r, 0.0)
            t2 = t * t
            w = (mb * (half + r)) * (t2 * t2)
            acc = acc + jnp.sum(w, axis=0)
        return acc

    halo_start(0, ext)
    lax.fori_loop(1, 1 + tc // edge, columns_step, 0)

    def self_step(s, carry):
        acc_ref[s] = pair_block(s, 0, edge + s, jnp.zeros((8, TILE), F32))
        return carry

    lax.fori_loop(0, tc, self_step, 0)
    halo_wait(0, ext)
    columns_step(0, 0)
    columns_step(1 + tc // edge, 0)

    def density_tile(s, keep):
        acc = acc_ref[s]
        for n in range(1, nb):
            acc = pair_block(s, n, near_ref[n, s] + base, acc, keep)
        h = ext[edge + s, 4:5, :]
        h2 = h * h
        h4 = h2 * h2
        value = jnp.sum(acc, axis=0, keepdims=True) * ((KERNEL_NORM / 8.0) / (h4 * h4))
        dens[edge + s] = value
        out_ref[1, pl.ds(s, 1), :] = value

    def edge_tile(q):
        return q + (tc - 2 * edge) * (q // edge)

    def density_edge(q, carry):
        density_tile(edge_tile(q), False)
        return carry

    def density_mid(q, carry):
        density_tile(q, True)
        return carry

    def force_mid(s, carry):
        for n in range(1, nb):
            force_block(s, n, near_ref[n, s] + base)
        return carry

    lax.fori_loop(0, 2 * edge, density_edge, 0)
    halo_start(1, dens)
    lax.fori_loop(edge, tc - edge, density_mid, 0)

    rows = lax.broadcasted_iota(jnp.int32, (8, TILE), 0)
    top = rows < 4

    def limiter_rows(sweep, j):
        lim[j] = split_rows(gv[j] * jnp.where(top, row(en[sweep, j]), 1.0))

    def start_tile(j):
        own = ext[j]
        one_x = jnp.where(lax.rem(rows, 4) == 0, 1.0, pltpu.roll(own, 1, 0) - SHIFT_X)
        two = jnp.where(top, one_x, pltpu.roll(one_x, 4, 0))
        volume = FORCE_NORM * own[3:4] / dens[j]
        vol[j] = volume
        gv[j] = two * row(volume)
        en[0, j] = own[5:6] - SHIFT_E
        limiter_rows(0, j)

    def jacobi_rows(sweep, j):
        vd = row(vol[j] * diff[sweep, j])
        pick = jnp.where(rows == 0, row(en[sweep, j]), jnp.where(rows == 1, 1.0, 0.0))
        jac[j] = split_rows(vd * pick)

    def start_step(j, carry):
        start_tile(j)
        return carry

    def product(table, s):
        parts = [table[edge + s]] + [table[near_ref[n, s] + base] for n in range(1, nb)]
        left_side = jnp.concatenate(parts, axis=1)
        right_side = jnp.concatenate(
            [force[k, pl.ds(s * nb, nb)].reshape(nb * TILE, TILE) for k in range(2)], axis=1
        )
        out = jnp.dot(left_side, right_side, preferred_element_type=F32)
        return (out[0:8, 0:TILE] + out[0:8, TILE:]) + (out[8:16, 0:TILE] + out[8:16, TILE:])

    def limiter_tile(sweep, s):
        value = product(lim, s)
        sums[s] = value
        e = en[sweep, edge + s]
        own = ext[edge + s]
        lead = value[0:1] - e * value[4:5]
        square = jnp.zeros((1, TILE), F32)
        for axis in range(3):
            g = value[1 + axis : 2 + axis] - e * value[5 + axis : 6 + axis]
            g = g - (own[axis : axis + 1] - SHIFT_X) * lead
            square = square + g * g
        opaque = own[6:7] * dens[edge + s]
        ratio = jnp.sqrt(square) / (opaque * (e + SHIFT_E))
        diff[sweep, edge + s] = (2.0 + ratio) / ((6.0 + 3.0 * ratio + ratio * ratio) * opaque)
        jacobi_rows(sweep, edge + s)

    def jacobi_tile(sweep, s):
        value = product(jac, s)
        own = ext[edge + s]
        old = sums[s]
        d = diff[sweep, edge + s]
        scale = TIME_STEP / dens[edge + s]
        inflow = d * old[0:1] + value[0:1]
        rate = d * old[4:5] + value[1:2]
        e = (own[5:6] - SHIFT_E + TIME_STEP * own[7:8] + scale * inflow) / (1.0 + scale * rate)
        if sweep == SWEEPS - 1:
            out_ref[0, pl.ds(s, 1), :] = e + SHIFT_E
        else:
            en[sweep + 1, edge + s] = e
            limiter_rows(sweep + 1, edge + s)

    flag = my_member // max(members - 1, 1)

    def edges(work, number=None, ref=None):
        lead = (tc - edge) * flag
        for k in range(edge):
            work(lead + k)
        if ref is not None:
            to_left, to_right = halo_copies(number, ref)
            pl.when(jnp.logical_and(has_left, flag == 0))(to_left.start)
            pl.when(jnp.logical_and(has_right, flag > 0))(to_right.start)
        for k in range(edge):
            work(tc - edge - lead + k)
        if ref is not None:
            pl.when(jnp.logical_and(has_right, flag == 0))(to_right.start)
            pl.when(jnp.logical_and(has_left, flag > 0))(to_left.start)

    def middle(work):
        for s in range(edge, tc - edge):
            work(s)

    def ghosts(work):
        for j in range(edge):
            work(j)
            work(edge + tc + j)

    lax.fori_loop(edge, edge + tc, start_step, 0)
    halo_wait(1, dens)
    ghosts(start_tile)

    for sweep in range(SWEEPS):
        if sweep > 0:
            halo_wait(2 * sweep + 1, en.at[sweep])
            ghosts(functools.partial(limiter_rows, sweep))
        work = functools.partial(limiter_tile, sweep)
        edges(work, 2 * sweep + 2, diff.at[sweep])
        if sweep == 0:
            lax.fori_loop(edge, tc - edge, force_mid, 0)
        middle(work)
        halo_wait(2 * sweep + 2, diff.at[sweep])
        ghosts(functools.partial(jacobi_rows, sweep))
        work = functools.partial(jacobi_tile, sweep)
        if sweep < SWEEPS - 1:
            edges(work, 2 * sweep + 3, en.at[sweep + 1])
        else:
            edges(work)
        middle(work)

    halo_done(0, ext)
    halo_done(1, dens)
    for sweep in range(SWEEPS):
        halo_done(2 * sweep + 2, diff.at[sweep])
        if sweep < SWEEPS - 1:
            halo_done(2 * sweep + 3, en.at[sweep + 1])


def solution(mesh):
    groups, members = mesh.shape["group"], mesh.shape["member"]

    def local(particles, new_slot, neighbours, ghosts):
        tc = new_slot.shape[0]
        nb = neighbours.shape[1]
        cap = max(2, (2 * tc + groups - 1) // groups)
        total = tc + 2 * GMAX
        halos = 2 + 2 * SWEEPS - 1
        vmem = pl.BlockSpec(memory_space=pltpu.VMEM)
        smem = pl.BlockSpec(memory_space=pltpu.SMEM)
        both = pl.pallas_call(
            functools.partial(kernel, groups, members, tc, nb, cap),
            out_shape=jax.ShapeDtypeStruct((2, tc, TILE), F32),
            in_specs=[vmem, smem, smem, smem],
            out_specs=vmem,
            scratch_shapes=[
                pltpu.VMEM((groups, cap + 1, 8, TILE), F32),
                pltpu.VMEM((groups, cap + 1, 8, TILE), F32),
                pltpu.VMEM((total, 8, TILE), F32),
                pltpu.VMEM((total, 5, TILE, TILE), F32),
                pltpu.VMEM((2, tc * nb, TILE, TILE), BF16),
                pltpu.VMEM((tc, 8, TILE), F32),
                pltpu.VMEM((total, 1, TILE), F32),
                pltpu.VMEM((total, 1, TILE), F32),
                pltpu.VMEM((total, 8, TILE), F32),
                pltpu.VMEM((SWEEPS, total, 1, TILE), F32),
                pltpu.VMEM((SWEEPS, total, 1, TILE), F32),
                pltpu.VMEM((total, 16, TILE), BF16),
                pltpu.VMEM((total, 16, TILE), BF16),
                pltpu.VMEM((tc, 8, TILE), F32),
                pltpu.VMEM(((tc - 2 * GMAX) * nb, TILE, TILE), F32),
                pltpu.SemaphoreType.DMA((groups,)),
                pltpu.SemaphoreType.DMA((groups,)),
                pltpu.SemaphoreType.DMA((halos, 2)),
                pltpu.SemaphoreType.DMA((halos, 2)),
            ],
            compiler_params=pltpu.CompilerParams(
                collective_id=0, has_side_effects=True, vmem_limit_bytes=60 * 1024 * 1024
            ),
        )(particles, new_slot, neighbours.T, ghosts)
        return both[0].reshape(-1), both[1].reshape(-1)

    in_specs = (
        P(None, ("group", "member")),
        P(("group", "member")),
        P(("group", "member"), None),
        P(("group", "member"), None),
    )
    out_specs = (P(("group", "member")), P(("group", "member")))
    return jax.shard_map(local, mesh=mesh, in_specs=in_specs, out_specs=out_specs, check_vma=False)
```
